32 devices in a mesh: members: 2 (over y), lat: 4 (over z), lev: 2 (over x), sub: 2 (over core).
Axes of the slice: x: 2, y: 2, z: 4, core: 2. Of those that a mesh axis runs over, the one named last changes fastest.
Arguments:
- thermal_state_grid: bfloat16 [272, 512, 1024], P(('members', 'lev', 'sub'), 'lat'), parts along dimension 0, may hold values from -6 to 6
- thermal_forcing: bfloat16 [272, 512, 1024], P(('members', 'lev', 'sub'), 'lat'), parts along dimension 0, may hold values from -6 to 6
- spherical_basis_table: bfloat16 [512, 512, 512], P(('lat', 'lev', 'sub')), may hold values from -0.25 to 0.25
- implicit_solver_matrix: bfloat16 [512, 136, 136], P(('lat', 'lev', 'sub')), may hold values from -0.5 to 0.5
- fourier_order_holder: int32 [512], replicated, may hold values from 0 to 511, as said below
Outputs:
- new_temperature: bfloat16 [272, 512, 1024], P(('members', 'lev', 'sub'), 'lat'), parts along dimension 0
The draws below stay inside these ranges and needn't reach their ends.
There are 2 independent parts, one for each index of `members`. The reference program is written for one: setup_inputs(seed, part) draws one part's arguments, and reference() takes and returns one part's arrays. A program takes and returns all parts, laid end to end along the dimension named above; an argument that names none is the same for every part. Nothing has to cross between parts.
Inputs may be any that keep to these rules, and one draw needn't show every extreme that they name: fourier_order_holder is a permutation of the waves; slots 2k and 2k+1 hold waves m and 511-m for some m.
All inputs are finite; a program needn't handle non-finite values.
Results may differ from the reference program's by a relative error of at most 0.0079.
Values may be sent and summed in bfloat16 or wider, within the bound.
A program may use at most 192 MiB of HBM per device.

```python
import math
import jax
import jax.numpy as jnp
from jax import lax

MERIDIAN_TOTAL = 1024
PARALLEL_TOTAL = 512
SIGMA_LAYERS = 136
M = 512


def draw_fourier_order_holder(key, part):
    half_count = M // 2
    pair_order = jax.random.permutation(key, half_count).astype(jnp.int32)
    flipped = jax.random.randint(jax.random.fold_in(key, 7), (half_count,), 0, 2).astype(jnp.int32)
    slot_ids = jnp.arange(M, dtype=jnp.int32)
    base_wave = pair_order[slot_ids // 2]
    leading = jnp.where(flipped[slot_ids // 2] == 1, M - 1 - base_wave, base_wave)
    is_second = slot_ids % 2
    return jnp.where(is_second == 1, M - 1 - leading, leading).astype(jnp.int32)


def shard_levels(rng, dims, split, smallest, largest):
    factor_of = 1.0
    for position, blocks in split:
        heights = jax.random.uniform(jax.random.fold_in(jax.random.fold_in(rng, 6), position), (blocks,), jnp.float32, smallest / len(split), largest / len(split))
        factor_of = factor_of * jnp.repeat(jnp.exp(heights), dims[position] // blocks).reshape((-1,) + (1,) * (len(dims) - 1 - position))
    return factor_of


def bell_draw(key, dims, deviation, bound, pieces=(), kind=jnp.bfloat16):
    loudness = shard_levels(key, dims, pieces, -0.22, 0.18) if pieces else 1.0
    array = jax.random.normal(key, dims, jnp.float32) * deviation * loudness
    return jnp.minimum(jnp.maximum(array, -bound), bound).astype(kind)


def setup_inputs(seed: int = 0, part: int = 0) -> dict:
    splits = jax.random.split(jax.random.key(seed), 6)
    part_splits = jax.random.split(jax.random.fold_in(splits[5], part), 6)
    thermal_state_grid = bell_draw(part_splits[0], (SIGMA_LAYERS, PARALLEL_TOTAL, MERIDIAN_TOTAL), 1.0, 6.0, ((0, 4), (1, 4)))
    thermal_forcing = bell_draw(part_splits[1], (SIGMA_LAYERS, PARALLEL_TOTAL, MERIDIAN_TOTAL), 1.0, 6.0, ((0, 4), (1, 4)))
    spherical_basis_table = bell_draw(splits[2], (M, PARALLEL_TOTAL, M), PARALLEL_TOTAL ** -0.5, 0.25, ((0, 16),))
    implicit_solver_matrix = bell_draw(splits[3], (M, SIGMA_LAYERS, SIGMA_LAYERS), SIGMA_LAYERS ** -0.5, 0.5, ((0, 16),))
    fourier_order_holder = draw_fourier_order_holder(jax.random.fold_in(splits[5], 71), part)
    return {"thermal_state_grid": thermal_state_grid, "thermal_forcing": thermal_forcing, "spherical_basis_table": spherical_basis_table, "implicit_solver_matrix": implicit_solver_matrix, "fourier_order_holder": fourier_order_holder}


block_slots = 16

def raw_table(fourier_order_holder, lon_count):
    meridian_position = jnp.arange(lon_count, dtype=jnp.int32)
    phases = meridian_position[:, None] * fourier_order_holder[None, :].astype(jnp.int32) % lon_count
    angles = phases.astype(jnp.float32) * (2.0 * math.pi / lon_count)
    factor = 1.0 / math.sqrt(lon_count)
    stacked = jnp.stack([jnp.cos(angles), -jnp.sin(angles)], axis=2)
    return stacked.reshape(lon_count, 2 * fourier_order_holder.shape[0]) * factor

def reference(thermal_state_grid, thermal_forcing, spherical_basis_table, implicit_solver_matrix, fourier_order_holder):
    present_state = thermal_state_grid.astype(jnp.float32)
    explicit = (present_state + 0.5 * thermal_forcing.astype(jnp.float32) - 0.3 * present_state * present_state * present_state / (1.0 + present_state * present_state)).astype(jnp.bfloat16)
    raw = raw_table(fourier_order_holder, MERIDIAN_TOTAL)
    analysis = raw.astype(jnp.bfloat16)
    weights = jnp.where(fourier_order_holder == 0, 1.0, 2.0).astype(jnp.float32)
    synthesis = (raw.T * jnp.repeat(weights, 2)[:, None]).astype(jnp.bfloat16)
    spectral = jnp.dot(explicit.reshape(SIGMA_LAYERS * PARALLEL_TOTAL, MERIDIAN_TOTAL), analysis, preferred_element_type=jnp.float32).astype(jnp.bfloat16)
    groups = M // block_slots
    spec_blocks = spectral.reshape(SIGMA_LAYERS, PARALLEL_TOTAL, groups, block_slots, 2).transpose(2, 0, 1, 3, 4)
    leg_blocks = spherical_basis_table.reshape(groups, block_slots, PARALLEL_TOTAL, M)

    def forward_group(operands):
        return jnp.einsum('lxsc,sxn->lscn', operands[0].astype(jnp.float32), operands[1].astype(jnp.float32)).astype(jnp.bfloat16)
    coeffs = lax.map(forward_group, (spec_blocks, leg_blocks))
    coeffs = coeffs.transpose(1, 0, 2, 3, 4).reshape(SIGMA_LAYERS, M, 2, M)
    solved = jnp.einsum('skl,lscn->kscn', implicit_solver_matrix.astype(jnp.float32), coeffs.astype(jnp.float32))
    degrees = jnp.arange(M, dtype=jnp.int32)
    live_mask = degrees[None, :] >= fourier_order_holder[:, None]
    solved = jnp.where(live_mask[None, :, None, :], solved, 0.0).astype(jnp.bfloat16)
    solved_blocks = solved.reshape(SIGMA_LAYERS, groups, block_slots, 2, M).transpose(1, 0, 2, 3, 4)

    def inverse_group(operands):
        return jnp.einsum('sxn,lscn->lxsc', operands[1].astype(jnp.float32), operands[0].astype(jnp.float32)).astype(jnp.bfloat16)
    synthesized = lax.map(inverse_group, (solved_blocks, leg_blocks))
    synthesized = synthesized.transpose(1, 2, 0, 3, 4).reshape(SIGMA_LAYERS * PARALLEL_TOTAL, 2 * M)
    result = jnp.dot(synthesized, synthesis, preferred_element_type=jnp.float32).astype(jnp.bfloat16)
    return result.reshape(SIGMA_LAYERS, PARALLEL_TOTAL, MERIDIAN_TOTAL)
```

```python
import math

import jax
import jax.numpy as jnp
from jax import lax
from jax.sharding import PartitionSpec as P

CHUNKS = 4
OWNERS = ("lat", "lev", "sub")


def raw_table(waves, lon_count):
    meridian = jnp.arange(lon_count, dtype=jnp.int32)
    phases = waves[:, None] * meridian[None, :] % lon_count
    angles = phases.astype(jnp.float32) * (2.0 * math.pi / lon_count)
    factor = 1.0 / math.sqrt(lon_count)
    return jnp.stack([jnp.cos(angles), -jnp.sin(angles)], axis=1) * factor


def make_shards(lat_parts, level_parts):
    owners = lat_parts * level_parts

    def shards(state, forcing, basis, solver, waves):
        levels, lats, lons = state.shape
        slots, lat_total, degrees = basis.shape
        level_total = solver.shape[1]
        present = state.astype(jnp.float32)
        explicit = (
            present
            + 0.5 * forcing.astype(jnp.float32)
            - 0.3 * present * present * present / (1.0 + present * present)
        ).astype(jnp.bfloat16)
        raw = raw_table(waves, lons)
        analysis = raw.astype(jnp.bfloat16)
        weights = jnp.where(waves == 0, 1.0, 2.0).astype(jnp.float32)
        synthesis = (raw * weights[:, None, None]).astype(jnp.bfloat16)
        chunks = CHUNKS
        part = slots // chunks
        analysis = analysis.reshape(owners, slots, 2, lons)
        synthesis = synthesis.reshape(owners, slots, 2, lons)
        owner = lax.axis_index(OWNERS)
        my_waves = lax.dynamic_slice_in_dim(waves, owner * slots, slots)
        live = jnp.arange(degrees, dtype=jnp.int32)[None, :] >= my_waves[:, None]
        sent = []
        for i in range(chunks):
            own = slice(i * part, (i + 1) * part)
            spectral = jnp.einsum(
                "oscj,lxj->osclx", analysis[:, own], explicit, preferred_element_type=jnp.float32
            ).astype(jnp.bfloat16)
            sent.append(lax.all_to_all(spectral, OWNERS, split_axis=0, concat_axis=0, tiled=True))
        back = []
        for i in range(chunks):
            own = slice(i * part, (i + 1) * part)
            got = sent[i].reshape(lat_parts, level_parts, part, 2, levels, lats)
            table = basis[own]
            columns = got.transpose(2, 3, 1, 4, 0, 5).reshape(part, 2 * level_total, lat_total)
            coeffs = jnp.einsum(
                "srx,sxn->srn", columns, table, preferred_element_type=jnp.float32
            ).astype(jnp.bfloat16).reshape(part, 2, level_total, degrees)
            solved = jnp.einsum(
                "skl,scln->sckn", solver[own], coeffs, preferred_element_type=jnp.float32
            )
            solved = jnp.where(live[own][:, None, None, :], solved, 0.0).astype(jnp.bfloat16)
            grid = jnp.einsum(
                "srn,sxn->srx",
                solved.reshape(part, 2 * level_total, degrees),
                table,
                preferred_element_type=jnp.float32,
            ).astype(jnp.bfloat16)
            grid = grid.reshape(part, 2, level_parts, levels, lat_parts, lats)
            grid = grid.transpose(4, 2, 0, 1, 3, 5).reshape(owners, part, 2, levels, lats)
            back.append(lax.all_to_all(grid, OWNERS, split_axis=0, concat_axis=0, tiled=True))
        waved = jnp.concatenate(back, axis=1)
        result = jnp.einsum(
            "osclx,oscj->lxj", waved, synthesis, preferred_element_type=jnp.float32
        )
        return result.astype(jnp.bfloat16)

    return shards


def solution(mesh):
    lat_parts = mesh.shape["lat"]
    level_parts = mesh.shape["lev"] * mesh.shape["sub"]
    return jax.shard_map(
        make_shards(lat_parts, level_parts),
        mesh=mesh,
        in_specs=(
            P(("members", "lev", "sub"), "lat", None),
            P(("members", "lev", "sub"), "lat", None),
            P(OWNERS, None, None),
            P(OWNERS, None, None),
            P(),
        ),
        out_specs=P(("members", "lev", "sub"), "lat", None),
        check_vma=False,
    )
```

```python
import functools
import math

import jax
import jax.numpy as jnp
from jax import lax
from jax.experimental import pallas as pl
from jax.experimental.pallas import tpu as pltpu
from jax.sharding import PartitionSpec as P

CHUNKS = 4
GROUP = 8
OWNERS = ("lat", "lev", "sub")


def raw_table(waves, lon_count):
    meridian = jnp.arange(lon_count, dtype=jnp.int32)
    phases = waves[:, None] * meridian[None, :] % lon_count
    angles = phases.astype(jnp.float32) * (2.0 * math.pi / lon_count)
    factor = 1.0 / math.sqrt(lon_count)
    return jnp.stack([jnp.cos(angles), -jnp.sin(angles)], axis=1) * factor


def place(peer, level_parts):
    subs = lax.axis_size("sub")
    return {
        "lat": peer // level_parts,
        "lev": (peer % level_parts) // subs,
        "sub": peer % subs,
    }


def my_place(level_parts):
    subs = lax.axis_size("sub")
    return lax.axis_index("lat") * level_parts + lax.axis_index("lev") * subs + lax.axis_index("sub")


def exchange(n, level_parts, last, piece, fill, send, out, send_sem, recv_sem, local_sem):
    mine = my_place(level_parts)

    def copy(peer, landing, cut):
        return pltpu.make_async_remote_copy(
            src_ref=send.at[(peer, *cut)],
            dst_ref=out.at[(landing, *cut)],
            send_sem=send_sem.at[peer],
            recv_sem=recv_sem.at[landing],
            device_id=place(peer, level_parts),
            device_id_type=pl.DeviceIdType.MESH,
        )

    def push(d, carry):
        peer = (mine + d) % n
        fill(peer)
        copy(peer, mine, (piece,)).start()
        return carry

    lax.fori_loop(1, n, push, 0)
    fill(mine)
    pltpu.make_async_copy(send.at[mine, piece], out.at[mine, piece], local_sem).start()

    @pl.when(last)
    def _():
        def settle(d, carry):
            peer = (mine + d) % n
            copy(peer, mine, ()).wait_send()
            copy(peer, peer, ()).wait_recv()
            return carry

        lax.fori_loop(1, n, settle, 0)
        pltpu.make_async_copy(send.at[mine], out.at[mine], local_sem).wait()


def greet(n, level_parts):
    mine = my_place(level_parts)
    barrier = pltpu.get_barrier_semaphore()

    def hello(d, carry):
        pl.semaphore_signal(
            barrier,
            inc=1,
            device_id=place((mine + d) % n, level_parts),
            device_id_type=pl.DeviceIdType.MESH,
        )
        return carry

    lax.fori_loop(1, n, hello, 0)
    pl.semaphore_wait(barrier, n - 1)


def dft_kernel(
    n, level_parts, steps,
    state, forcing, near, far, out, synthesis, table, send, send_sem, recv_sem, local_sem,
):
    step = pl.program_id(0)
    levels, lats, lons = state.shape
    tile = near.shape[2]

    def trig(a):
        return far[0, :, a : a + 1] * near[0] - far[1, :, a : a + 1] * near[1]

    @pl.when(step == 0)
    def _():
        for a in range(lons // tile):
            table[:, a * tile : (a + 1) * tile] = trig(a).astype(jnp.bfloat16)
        greet(n, level_parts)

    present = state[...].astype(jnp.float32)
    explicit = (
        present
        + 0.5 * forcing[...].astype(jnp.float32)
        - 0.3 * present * present * present / (1.0 + present * present)
    ).astype(jnp.bfloat16)
    spectral = lax.dot_general(
        table[...],
        explicit.reshape(levels * lats, lons),
        (((1,), (1,)), ((), ())),
        preferred_element_type=jnp.float32,
    ).astype(jnp.bfloat16)
    spectral = spectral.reshape(n, -1, levels * lats)
    for level in range(levels):
        send[:, step * levels + level] = spectral[:, :, level * lats : (level + 1) * lats]

    @pl.when(step == steps - 1)
    def _():
        for a in range(lons // tile):
            synthesis[:, a * tile : (a + 1) * tile] = (
                trig(a) * far[2, :, a : a + 1]
            ).astype(jnp.bfloat16)

    exchange(
        n, level_parts, step == steps - 1, pl.ds(step * levels, levels), lambda peer: None,
        send, out, send_sem, recv_sem, local_sem,
    )


def dft_exchange(state, forcing, near, far, n, level_parts):
    levels, lats, lons = state.shape
    rows = near.shape[1]
    few = 2
    steps = levels // few
    shape = (n, levels, rows // n, lats)
    grid_block = pl.BlockSpec((few, lats, lons), lambda i: (i, 0, 0))
    return pl.pallas_call(
        functools.partial(dft_kernel, n, level_parts, steps),
        out_shape=(
            jax.ShapeDtypeStruct(shape, jnp.bfloat16),
            jax.ShapeDtypeStruct((rows, lons), jnp.bfloat16),
        ),
        grid=(steps,),
        in_specs=[
            grid_block,
            grid_block,
            pl.BlockSpec(near.shape, lambda i: (0, 0, 0)),
            pl.BlockSpec(far.shape, lambda i: (0, 0, 0)),
        ],
        out_specs=(
            pl.BlockSpec(memory_space=pl.ANY),
            pl.BlockSpec((rows, lons), lambda i: (0, 0)),
        ),
        scratch_shapes=[
            pltpu.VMEM((rows, lons), jnp.bfloat16),
            pltpu.VMEM(shape, jnp.bfloat16),
            pltpu.SemaphoreType.DMA((n,)),
            pltpu.SemaphoreType.DMA((n,)),
            pltpu.SemaphoreType.DMA,
        ],
        compiler_params=pltpu.CompilerParams(
            collective_id=0, has_side_effects=True, vmem_limit_bytes=48 << 20
        ),
    )(state, forcing, near, far)


def small_tables(waves, lon_count, tile):
    waves = jnp.repeat(waves, 2)[:, None]
    quarter = (jnp.arange(waves.shape[0], dtype=jnp.int32) % 2)[:, None] * (lon_count // 4)
    unit = 2.0 * math.pi / lon_count
    fine = jnp.arange(tile, dtype=jnp.int32)[None, :] * waves % lon_count
    coarse = jnp.arange(lon_count // tile, dtype=jnp.int32)[None, :] * tile * waves + quarter
    fine, coarse = fine.astype(jnp.float32) * unit, (coarse % lon_count).astype(jnp.float32) * unit
    factor = 1.0 / math.sqrt(lon_count)
    weights = jnp.broadcast_to(jnp.where(waves == 0, 1.0, 2.0), coarse.shape)
    near = jnp.stack([jnp.cos(fine), jnp.sin(fine)])
    far = jnp.stack([jnp.cos(coarse) * factor, jnp.sin(coarse) * factor, weights])
    return near, far


def columns_of_chunk(n, level_parts, levels, lats, got, basis, solver, live, wide, rows, mix, split):
    lat_parts = n // level_parts
    total = levels * level_parts
    pairs = 2 * GROUP

    def gather(q, carry):
        lanes = pl.ds(pl.multiple_of(q * lats, lats), lats)
        for g in range(level_parts):
            wide[g] = got[q * level_parts + g].astype(jnp.float32).reshape(levels * pairs, lats)
            for k in range(pairs):
                rows[k, pl.ds(g * levels, levels), lanes] = wide[g, pl.ds(k, levels, stride=pairs), :]
        return carry

    lax.fori_loop(0, lat_parts, gather, 0)

    def slot(s, carry):
        table = basis[s]
        packed = rows[pl.ds(2 * s, 2)].reshape(2 * total, lat_parts * lats).astype(jnp.bfloat16)
        coeffs = jnp.dot(packed, table, preferred_element_type=jnp.float32)
        mask = live[s] > 0.5
        solved = []
        for c in range(2):
            part = coeffs[c * total : (c + 1) * total].astype(jnp.bfloat16)
            part = jnp.dot(solver[s], part, preferred_element_type=jnp.float32)
            solved.append(jnp.where(mask, part, 0.0))
        solved = jnp.concatenate(solved, axis=0).astype(jnp.bfloat16)
        mix[...] = lax.dot_general(
            solved, table, (((1,), (1,)), ((), ())), preferred_element_type=jnp.float32
        )
        for q in range(lat_parts):
            for g in range(level_parts):
                for c in range(2):
                    split[q * level_parts + g, pl.ds(2 * s + c, levels, stride=pairs), :] = mix[
                        pl.ds(c * total + g * levels, levels), q * lats : (q + 1) * lats
                    ]
        return carry

    lax.fori_loop(0, GROUP, slot, 0)


def middle_kernel(
    n, level_parts, levels, lats, steps,
    got, basis, solver, live, out, wide, rows, mix, split, send, send_sem, recv_sem, local_sem,
):
    step = pl.program_id(0)

    @pl.when(step == 0)
    def _():
        greet(n, level_parts)

    columns_of_chunk(n, level_parts, levels, lats, got, basis, solver, live, wide, rows, mix, split)

    def fill(peer):
        send[peer, step] = split[peer].astype(jnp.bfloat16)

    exchange(
        n, level_parts, step == steps - 1, step, fill,
        send, out, send_sem, recv_sem, local_sem,
    )


def middle(got, basis, solver, live, n, level_parts):
    _, levels, _, lats = got.shape
    slots, lat_total, degrees = basis.shape
    total = solver.shape[1]
    pairs = 2 * GROUP
    steps, span = slots // GROUP, levels * pairs
    shape = (n, steps, span, lats)
    return pl.pallas_call(
        functools.partial(middle_kernel, n, level_parts, levels, lats, steps),
        out_shape=jax.ShapeDtypeStruct(shape, jnp.bfloat16),
        grid=(steps,),
        in_specs=[
            pl.BlockSpec((n, levels, pairs, lats), lambda i: (0, 0, i, 0)),
            pl.BlockSpec((GROUP, lat_total, degrees), lambda i: (i, 0, 0)),
            pl.BlockSpec((GROUP, total, total), lambda i: (i, 0, 0)),
            pl.BlockSpec((GROUP, 1, degrees), lambda i: (i, 0, 0)),
        ],
        out_specs=pl.BlockSpec(memory_space=pl.ANY),
        scratch_shapes=[
            pltpu.VMEM((level_parts, span, lats), jnp.float32),
            pltpu.VMEM((pairs, total, lat_total), jnp.float32),
            pltpu.VMEM((2 * total, lat_total), jnp.float32),
            pltpu.VMEM((n, span, lats), jnp.float32),
            pltpu.VMEM(shape, jnp.bfloat16),
            pltpu.SemaphoreType.DMA((n,)),
            pltpu.SemaphoreType.DMA((n,)),
            pltpu.SemaphoreType.DMA,
        ],
        compiler_params=pltpu.CompilerParams(
            collective_id=1, has_side_effects=True, vmem_limit_bytes=52 << 20
        ),
    )(got, basis, solver, live)


def make_shards(lat_parts, level_parts):
    owners = lat_parts * level_parts

    def shards(state, forcing, basis, solver, waves):
        levels, lats, lons = state.shape
        slots, lat_total, degrees = basis.shape
        level_total = solver.shape[1]
        owner = lax.axis_index(OWNERS)
        my_waves = lax.dynamic_slice_in_dim(waves, owner * slots, slots)
        live = jnp.arange(degrees, dtype=jnp.int32)[None, :] >= my_waves[:, None]
        if lats % 128 == 0 and lons % 512 == 0 and slots % GROUP == 0 and levels % 2 == 0:
            near, far = small_tables(waves, lons, 128)
            got, synthesis = dft_exchange(state, forcing, near, far, owners, level_parts)
            alive = live.astype(jnp.float32)[:, None, :]
            back = middle(got, basis, solver, alive, owners, level_parts)
            waved = back.reshape(owners, slots // GROUP, levels, 2 * GROUP, lats)
            synthesis = synthesis.reshape(owners, slots // GROUP, 2 * GROUP, lons)
            result = jnp.einsum(
                "ohlkx,ohkj->lxj", waved, synthesis, preferred_element_type=jnp.float32
            )
            return result.astype(jnp.bfloat16)
        present = state.astype(jnp.float32)
        explicit = (
            present
            + 0.5 * forcing.astype(jnp.float32)
            - 0.3 * present * present * present / (1.0 + present * present)
        ).astype(jnp.bfloat16)
        raw = raw_table(waves, lons)
        analysis = raw.astype(jnp.bfloat16)
        weights = jnp.where(waves == 0, 1.0, 2.0).astype(jnp.float32)
        synthesis = (raw * weights[:, None, None]).astype(jnp.bfloat16)
        chunks = CHUNKS
        part = slots // chunks
        analysis = analysis.reshape(owners, slots, 2, lons)
        synthesis = synthesis.reshape(owners, slots, 2, lons)
        sent = []
        for i in range(chunks):
            own = slice(i * part, (i + 1) * part)
            spectral = jnp.einsum(
                "oscj,lxj->osclx", analysis[:, own], explicit, preferred_element_type=jnp.float32
            ).astype(jnp.bfloat16)
            sent.append(lax.all_to_all(spectral, OWNERS, split_axis=0, concat_axis=0, tiled=True))
        back = []
        for i in range(chunks):
            own = slice(i * part, (i + 1) * part)
            got = sent[i].reshape(lat_parts, level_parts, part, 2, levels, lats)
            table = basis[own]
            columns = got.transpose(2, 3, 1, 4, 0, 5).reshape(part, 2 * level_total, lat_total)
            coeffs = jnp.einsum(
                "srx,sxn->srn", columns, table, preferred_element_type=jnp.float32
            ).astype(jnp.bfloat16).reshape(part, 2, level_total, degrees)
            solved = jnp.einsum(
                "skl,scln->sckn", solver[own], coeffs, preferred_element_type=jnp.float32
            )
            solved = jnp.where(live[own][:, None, None, :], solved, 0.0).astype(jnp.bfloat16)
            grid = jnp.einsum(
                "srn,sxn->srx",
                solved.reshape(part, 2 * level_total, degrees),
                table,
                preferred_element_type=jnp.float32,
            ).astype(jnp.bfloat16)
            grid = grid.reshape(part, 2, level_parts, levels, lat_parts, lats)
            grid = grid.transpose(4, 2, 0, 1, 3, 5).reshape(owners, part, 2, levels, lats)
            back.append(lax.all_to_all(grid, OWNERS, split_axis=0, concat_axis=0, tiled=True))
        waved = jnp.concatenate(back, axis=1)
        result = jnp.einsum(
            "osclx,oscj->lxj", waved, synthesis, preferred_element_type=jnp.float32
        )
        return result.astype(jnp.bfloat16)

    return shards


def solution(mesh):
    lat_parts = mesh.shape["lat"]
    level_parts = mesh.shape["lev"] * mesh.shape["sub"]
    return jax.shard_map(
        make_shards(lat_parts, level_parts),
        mesh=mesh,
        in_specs=(
            P(("members", "lev", "sub"), "lat", None),
            P(("members", "lev", "sub"), "lat", None),
            P(OWNERS, None, None),
            P(OWNERS, None, None),
            P(),
        ),
        out_specs=P(("members", "lev", "sub"), "lat", None),
        check_vma=False,
    )
```

```python
import functools
import math

import jax
import jax.numpy as jnp
from jax import lax
from jax.experimental import pallas as pl
from jax.experimental.pallas import tpu as pltpu
from jax.sharding import PartitionSpec as P

CHUNKS = 4
GROUP = 8
OWNERS = ("lat", "lev", "sub")


def raw_table(waves, lon_count):
    meridian = jnp.arange(lon_count, dtype=jnp.int32)
    phases = waves[:, None] * meridian[None, :] % lon_count
    angles = phases.astype(jnp.float32) * (2.0 * math.pi / lon_count)
    factor = 1.0 / math.sqrt(lon_count)
    return jnp.stack([jnp.cos(angles), -jnp.sin(angles)], axis=1) * factor


def place(peer, level_parts):
    subs = lax.axis_size("sub")
    return {
        "lat": peer // level_parts,
        "lev": (peer % level_parts) // subs,
        "sub": peer % subs,
    }


def my_place(level_parts):
    subs = lax.axis_size("sub")
    return lax.axis_index("lat") * level_parts + lax.axis_index("lev") * subs + lax.axis_index("sub")


def exchange(n, level_parts, last, piece, fill, send, out, send_sem, recv_sem, local_sem):
    mine = my_place(level_parts)

    def copy(peer, landing, cut):
        return pltpu.make_async_remote_copy(
            src_ref=send.at[(peer, *cut)],
            dst_ref=out.at[(landing, *cut)],
            send_sem=send_sem.at[peer],
            recv_sem=recv_sem.at[landing],
            device_id=place(peer, level_parts),
            device_id_type=pl.DeviceIdType.MESH,
        )

    lat_parts = n // level_parts
    lat, group, sub = mine // level_parts, mine % level_parts, lax.axis_index("sub")

    def push(t, carry):
        turn = (lat + t // level_parts + (1 - sub) * (lat_parts // 2)) % lat_parts
        peer = turn * level_parts + (group + t) % level_parts
        fill(peer)

        @pl.when(peer != mine)
        def _():
            copy(peer, mine, (piece,)).start()

        return carry

    lax.fori_loop(0, n, push, 0)
    pltpu.make_async_copy(send.at[mine, piece], out.at[mine, piece], local_sem).start()

    @pl.when(last)
    def _():
        def settle(d, carry):
            peer = (mine + d) % n
            copy(peer, mine, ()).wait_send()
            copy(peer, peer, ()).wait_recv()
            return carry

        lax.fori_loop(1, n, settle, 0)
        pltpu.make_async_copy(send.at[mine], out.at[mine], local_sem).wait()


def greet(n, level_parts):
    mine = my_place(level_parts)
    barrier = pltpu.get_barrier_semaphore()

    def hello(d, carry):
        pl.semaphore_signal(
            barrier,
            inc=1,
            device_id=place((mine + d) % n, level_parts),
            device_id_type=pl.DeviceIdType.MESH,
        )
        return carry

    lax.fori_loop(1, n, hello, 0)


def dft_kernel(
    n, level_parts, steps,
    state, forcing, near, far, out, synthesis, table, send, send_sem, recv_sem, local_sem,
):
    step = pl.program_id(0)
    levels, lats, lons = state.shape
    tile = near.shape[2]

    def trig(a):
        return far[0, :, a : a + 1] * near[0] - far[1, :, a : a + 1] * near[1]

    @pl.when(step == 0)
    def _():
        greet(n, level_parts)
        for a in range(lons // tile):
            table[:, a * tile : (a + 1) * tile] = trig(a).astype(jnp.bfloat16)

    present = state[...].astype(jnp.float32)
    explicit = (
        present
        + 0.5 * forcing[...].astype(jnp.float32)
        - 0.3 * present * present * present / (1.0 + present * present)
    ).astype(jnp.bfloat16)
    spectral = lax.dot_general(
        table[...],
        explicit.reshape(levels * lats, lons),
        (((1,), (1,)), ((), ())),
        preferred_element_type=jnp.float32,
    ).astype(jnp.bfloat16)

    @pl.when(step == 0)
    def _():
        pl.semaphore_wait(pltpu.get_barrier_semaphore(), n - 1)

    spectral = spectral.reshape(n, -1, levels * lats)
    for level in range(levels):
        send[:, step * levels + level] = spectral[:, :, level * lats : (level + 1) * lats]

    @pl.when(step == steps - 1)
    def _():
        for a in range(lons // tile):
            synthesis[:, a * tile : (a + 1) * tile] = (
                trig(a) * far[2, :, a : a + 1]
            ).astype(jnp.bfloat16)

    exchange(
        n, level_parts, step == steps - 1, pl.ds(step * levels, levels), lambda peer: None,
        send, out, send_sem, recv_sem, local_sem,
    )


def dft_exchange(state, forcing, near, far, n, level_parts):
    levels, lats, lons = state.shape
    rows = near.shape[1]
    few = 2
    steps = levels // few
    shape = (n, levels, rows // n, lats)
    grid_block = pl.BlockSpec((few, lats, lons), lambda i: (i, 0, 0))
    return pl.pallas_call(
        functools.partial(dft_kernel, n, level_parts, steps),
        out_shape=(
            jax.ShapeDtypeStruct(shape, jnp.bfloat16),
            jax.ShapeDtypeStruct((rows, lons), jnp.bfloat16),
        ),
        grid=(steps,),
        in_specs=[
            grid_block,
            grid_block,
            pl.BlockSpec(near.shape, lambda i: (0, 0, 0)),
            pl.BlockSpec(far.shape, lambda i: (0, 0, 0)),
        ],
        out_specs=(
            pl.BlockSpec(memory_space=pl.ANY),
            pl.BlockSpec((rows, lons), lambda i: (0, 0)),
        ),
        scratch_shapes=[
            pltpu.VMEM((rows, lons), jnp.bfloat16),
            pltpu.VMEM(shape, jnp.bfloat16),
            pltpu.SemaphoreType.DMA((n,)),
            pltpu.SemaphoreType.DMA((n,)),
            pltpu.SemaphoreType.DMA,
        ],
        compiler_params=pltpu.CompilerParams(
            collective_id=0, has_side_effects=True, vmem_limit_bytes=48 << 20
        ),
    )(state, forcing, near, far)


def small_tables(waves, lon_count, tile):
    waves = jnp.repeat(waves, 2)[:, None]
    quarter = (jnp.arange(waves.shape[0], dtype=jnp.int32) % 2)[:, None] * (lon_count // 4)
    unit = 2.0 * math.pi / lon_count
    fine = jnp.arange(tile, dtype=jnp.int32)[None, :] * waves % lon_count
    coarse = jnp.arange(lon_count // tile, dtype=jnp.int32)[None, :] * tile * waves + quarter
    fine, coarse = fine.astype(jnp.float32) * unit, (coarse % lon_count).astype(jnp.float32) * unit
    factor = 1.0 / math.sqrt(lon_count)
    weights = jnp.broadcast_to(jnp.where(waves == 0, 1.0, 2.0), coarse.shape)
    near = jnp.stack([jnp.cos(fine), jnp.sin(fine)])
    far = jnp.stack([jnp.cos(coarse) * factor, jnp.sin(coarse) * factor, weights])
    return near, far


def columns_of_chunk(n, level_parts, levels, lats, got, basis, solver, live, wide, rows, mix, split):
    lat_parts = n // level_parts
    total = levels * level_parts
    pairs = 2 * GROUP

    def gather(q, carry):
        lanes = pl.ds(pl.multiple_of(q * lats, lats), lats)
        for g in range(level_parts):
            wide[g] = got[q * level_parts + g].astype(jnp.float32).reshape(levels * pairs, lats)
            for k in range(pairs):
                rows[k, pl.ds(g * levels, levels), lanes] = wide[g, pl.ds(k, levels, stride=pairs), :]
        return carry

    lax.fori_loop(0, lat_parts, gather, 0)

    def slot(s, carry):
        table = basis[s]
        packed = rows[pl.ds(2 * s, 2)].reshape(2 * total, lat_parts * lats).astype(jnp.bfloat16)
        coeffs = jnp.dot(packed, table, preferred_element_type=jnp.float32)
        mask = live[s] > 0.5
        solved = []
        for c in range(2):
            part = coeffs[c * total : (c + 1) * total].astype(jnp.bfloat16)
            part = jnp.dot(solver[s], part, preferred_element_type=jnp.float32)
            solved.append(jnp.where(mask, part, 0.0))
        solved = jnp.concatenate(solved, axis=0).astype(jnp.bfloat16)
        mix[...] = lax.dot_general(
            solved, table, (((1,), (1,)), ((), ())), preferred_element_type=jnp.float32
        )
        for q in range(lat_parts):
            for g in range(level_parts):
                for c in range(2):
                    split[q * level_parts + g, pl.ds(2 * s + c, levels, stride=pairs), :] = mix[
                        pl.ds(c * total + g * levels, levels), q * lats : (q + 1) * lats
                    ]
        return carry

    lax.fori_loop(0, GROUP, slot, 0)


def middle_kernel(
    n, level_parts, levels, lats, steps,
    got, basis, solver, live, out, wide, rows, mix, split, send, send_sem, recv_sem, local_sem,
):
    step = pl.program_id(0)

    @pl.when(step == 0)
    def _():
        greet(n, level_parts)

    columns_of_chunk(n, level_parts, levels, lats, got, basis, solver, live, wide, rows, mix, split)

    @pl.when(step == 0)
    def _():
        pl.semaphore_wait(pltpu.get_barrier_semaphore(), n - 1)

    def fill(peer):
        send[peer, step] = split[peer].astype(jnp.bfloat16)

    exchange(
        n, level_parts, step == steps - 1, step, fill,
        send, out, send_sem, recv_sem, local_sem,
    )


def middle(got, basis, solver, live, n, level_parts):
    _, levels, _, lats = got.shape
    slots, lat_total, degrees = basis.shape
    total = solver.shape[1]
    pairs = 2 * GROUP
    steps, span = slots // GROUP, levels * pairs
    shape = (n, steps, span, lats)
    return pl.pallas_call(
        functools.partial(middle_kernel, n, level_parts, levels, lats, steps),
        out_shape=jax.ShapeDtypeStruct(shape, jnp.bfloat16),
        grid=(steps,),
        in_specs=[
            pl.BlockSpec((n, levels, pairs, lats), lambda i: (0, 0, i, 0)),
            pl.BlockSpec((GROUP, lat_total, degrees), lambda i: (i, 0, 0)),
            pl.BlockSpec((GROUP, total, total), lambda i: (i, 0, 0)),
            pl.BlockSpec((GROUP, 1, degrees), lambda i: (i, 0, 0)),
        ],
        out_specs=pl.BlockSpec(memory_space=pl.ANY),
        scratch_shapes=[
            pltpu.VMEM((level_parts, span, lats), jnp.float32),
            pltpu.VMEM((pairs, total, lat_total), jnp.float32),
            pltpu.VMEM((2 * total, lat_total), jnp.float32),
            pltpu.VMEM((n, span, lats), jnp.float32),
            pltpu.VMEM(shape, jnp.bfloat16),
            pltpu.SemaphoreType.DMA((n,)),
            pltpu.SemaphoreType.DMA((n,)),
            pltpu.SemaphoreType.DMA,
        ],
        compiler_params=pltpu.CompilerParams(
            collective_id=1, has_side_effects=True, vmem_limit_bytes=52 << 20
        ),
    )(got, basis, solver, live)


def make_shards(lat_parts, level_parts):
    owners = lat_parts * level_parts

    def shards(state, forcing, basis, solver, waves):
        levels, lats, lons = state.shape
        slots, lat_total, degrees = basis.shape
        level_total = solver.shape[1]
        owner = lax.axis_index(OWNERS)
        my_waves = lax.dynamic_slice_in_dim(waves, owner * slots, slots)
        live = jnp.arange(degrees, dtype=jnp.int32)[None, :] >= my_waves[:, None]
        if lats % 128 == 0 and lons % 512 == 0 and slots % GROUP == 0 and levels % 2 == 0:
            near, far = small_tables(waves, lons, 128)
            got, synthesis = dft_exchange(state, forcing, near, far, owners, level_parts)
            alive = live.astype(jnp.float32)[:, None, :]
            back = middle(got, basis, solver, alive, owners, level_parts)
            waved = back.reshape(owners, slots // GROUP, levels, 2 * GROUP, lats)
            synthesis = synthesis.reshape(owners, slots // GROUP, 2 * GROUP, lons)
            result = jnp.einsum(
                "ohlkx,ohkj->lxj", waved, synthesis, preferred_element_type=jnp.float32
            )
            return result.astype(jnp.bfloat16)
        present = state.astype(jnp.float32)
        explicit = (
            present
            + 0.5 * forcing.astype(jnp.float32)
            - 0.3 * present * present * present / (1.0 + present * present)
        ).astype(jnp.bfloat16)
        raw = raw_table(waves, lons)
        analysis = raw.astype(jnp.bfloat16)
        weights = jnp.where(waves == 0, 1.0, 2.0).astype(jnp.float32)
        synthesis = (raw * weights[:, None, None]).astype(jnp.bfloat16)
        chunks = CHUNKS
        part = slots // chunks
        analysis = analysis.reshape(owners, slots, 2, lons)
        synthesis = synthesis.reshape(owners, slots, 2, lons)
        sent = []
        for i in range(chunks):
            own = slice(i * part, (i + 1) * part)
            spectral = jnp.einsum(
                "oscj,lxj->osclx", analysis[:, own], explicit, preferred_element_type=jnp.float32
            ).astype(jnp.bfloat16)
            sent.append(lax.all_to_all(spectral, OWNERS, split_axis=0, concat_axis=0, tiled=True))
        back = []
        for i in range(chunks):
            own = slice(i * part, (i + 1) * part)
            got = sent[i].reshape(lat_parts, level_parts, part, 2, levels, lats)
            table = basis[own]
            columns = got.transpose(2, 3, 1, 4, 0, 5).reshape(part, 2 * level_total, lat_total)
            coeffs = jnp.einsum(
                "srx,sxn->srn", columns, table, preferred_element_type=jnp.float32
            ).astype(jnp.bfloat16).reshape(part, 2, level_total, degrees)
            solved = jnp.einsum(
                "skl,scln->sckn", solver[own], coeffs, preferred_element_type=jnp.float32
            )
            solved = jnp.where(live[own][:, None, None, :], solved, 0.0).astype(jnp.bfloat16)
            grid = jnp.einsum(
                "srn,sxn->srx",
                solved.reshape(part, 2 * level_total, degrees),
                table,
                preferred_element_type=jnp.float32,
            ).astype(jnp.bfloat16)
            grid = grid.reshape(part, 2, level_parts, levels, lat_parts, lats)
            grid = grid.transpose(4, 2, 0, 1, 3, 5).reshape(owners, part, 2, levels, lats)
            back.append(lax.all_to_all(grid, OWNERS, split_axis=0, concat_axis=0, tiled=True))
        waved = jnp.concatenate(back, axis=1)
        result = jnp.einsum(
            "osclx,oscj->lxj", waved, synthesis, preferred_element_type=jnp.float32
        )
        return result.astype(jnp.bfloat16)

    return shards


def solution(mesh):
    lat_parts = mesh.shape["lat"]
    level_parts = mesh.shape["lev"] * mesh.shape["sub"]
    return jax.shard_map(
        make_shards(lat_parts, level_parts),
        mesh=mesh,
        in_specs=(
            P(("members", "lev", "sub"), "lat", None),
            P(("members", "lev", "sub"), "lat", None),
            P(OWNERS, None, None),
            P(OWNERS, None, None),
            P(),
        ),
        out_specs=P(("members", "lev", "sub"), "lat", None),
        check_vma=False,
    )
```
